32 devices in a mesh: section: 4 (over z), ctx: 8 (over y, x, core).
Axes of the slice: x: 2, y: 2, z: 4, core: 2. Of those that a mesh axis runs over, the one named last changes fastest.
Arguments:
- gate_rows: bfloat16 [4, 1024, 4096], P('section', 'ctx'), may hold values from -6 to 6
- key_rows: bfloat16 [4, 1024, 4096], P('section', 'ctx'), may hold values from -6 to 6
- value_rows: bfloat16 [4, 1024, 4096], P('section', 'ctx'), may hold values from -6 to 6
- filters: bfloat16 [4, 1024, 256], P('section', 'ctx'), may hold values from -1.1 to 1.1
- skip_gain: float32 [4096], replicated, may hold values from -3 to 3
Outputs:
- passed: bfloat16 [4, 1024, 4096], P('section', 'ctx')
The draws below stay inside these ranges and needn't reach their ends.
All inputs are finite; a program needn't handle non-finite values.
Results may differ from the reference program's by a relative error of at most 0.007.
Values may be sent and summed in bfloat16 or wider, within the bound.
A program may use at most 64 MiB of HBM per device.

```python
import math
import jax
import jax.numpy as jnp
from jax import lax

C = 4096
LONG_FILTERS = 256
SEQUENCE_LENGTH = 1024
RELAY_SECTIONS = 4


def draw_filters(key, part):
    frequency_key, jitter_key, spike_key = jax.random.split(key, 3)
    position_grid = jnp.arange(SEQUENCE_LENGTH, dtype=jnp.float32)[None, :, None]
    decay_log = jax.random.uniform(frequency_key, (RELAY_SECTIONS, 1, LONG_FILTERS), minval=math.log(30.0), maxval=math.log(4 * SEQUENCE_LENGTH))
    noise_draw = jax.random.truncated_normal(jitter_key, -4.0, 4.0, (RELAY_SECTIONS, SEQUENCE_LENGTH, LONG_FILTERS))
    decay_len = jnp.exp(decay_log)
    spike_events = jax.random.randint(spike_key, (3, RELAY_SECTIONS, 1, LONG_FILTERS), 0, SEQUENCE_LENGTH)
    multiplier_amount = jnp.ones((RELAY_SECTIONS, SEQUENCE_LENGTH, LONG_FILTERS), jnp.float32)
    for spike_location in range(3):
        multiplier_amount = multiplier_amount * jnp.where(position_grid >= spike_events[spike_location].astype(jnp.float32), 0.6, 1.0)
    values = noise_draw * jnp.sqrt(2.0 / decay_len) * jnp.exp(-position_grid / decay_len) * multiplier_amount
    return values.astype(jnp.bfloat16)


def shard_levels(own_key, extent, cuts, least, high):
    def one(dim, parts):
        heights = jax.random.uniform(jax.random.fold_in(jax.random.fold_in(own_key, 6), dim), (parts,), jnp.float32, least / len(cuts), high / len(cuts))
        return jnp.repeat(jnp.exp(heights), extent[dim] // parts).reshape((-1,) + (1,) * (len(extent) - dim - 1))

    level = one(*cuts[0])
    for cut in cuts[1:]:
        level = level * one(*cut)
    return level


def gaussian(own_key, shape, deviation, bound, pieces=(), kind=jnp.bfloat16):
    entries = deviation * jax.random.normal(own_key, shape, jnp.float32)
    if pieces:
        entries = entries * shard_levels(own_key, shape, pieces, -0.22, 0.18)
    return jnp.clip(entries, -bound, bound).astype(kind)


def setup_inputs(seed: int = 0) -> dict:
    keys = jax.random.split(jax.random.key(seed), 6)
    return {
        "gate_rows": gaussian(keys[0], (RELAY_SECTIONS, SEQUENCE_LENGTH, C), 1.0, 6.0, ((0, 4), (1, 8))),
        "key_rows": gaussian(keys[1], (RELAY_SECTIONS, SEQUENCE_LENGTH, C), 1.0, 6.0, ((0, 4), (1, 8))),
        "value_rows": gaussian(keys[2], (RELAY_SECTIONS, SEQUENCE_LENGTH, C), 1.0, 6.0, ((0, 4), (1, 8))),
        "filters": draw_filters(jax.random.fold_in(keys[5], 71), 0),
        "skip_gain": gaussian(keys[4], (C,), 0.5, 3.0, (), jnp.float32),
    }


def section_layer(gate_part, key_part, value_part, filter_rows, skip_gain):
    mixed = (key_part.astype(jnp.float32) * value_part.astype(jnp.float32)).astype(jnp.bfloat16)
    mixed = lax.optimization_barrier(mixed).astype(jnp.float32)
    fft_length = 2 * SEQUENCE_LENGTH
    filter_spec = jnp.fft.rfft(filter_rows.astype(jnp.float32), n=fft_length, axis=0)
    block_width = 2 * LONG_FILTERS
    block_starts = jnp.arange(C // block_width, dtype=jnp.int32) * block_width

    def one_block(start_col):
        channel_slab = lax.dynamic_slice_in_dim(mixed, start_col.astype(jnp.int32), block_width, axis=1)
        slab_spec = jnp.fft.rfft(channel_slab, n=fft_length, axis=0) * jnp.tile(filter_spec, (1, 2))
        return jnp.fft.irfft(slab_spec, n=fft_length, axis=0)[:SEQUENCE_LENGTH]

    conv_blocks = lax.map(one_block, block_starts)
    convolved = jnp.transpose(conv_blocks, (1, 0, 2)).reshape(SEQUENCE_LENGTH, C)
    return (gate_part.astype(jnp.float32) * (convolved + skip_gain[None, :] * mixed)).astype(jnp.bfloat16)


def reference(gate_rows, key_rows, value_rows, filters, skip_gain):
    outputs = []
    for section_pos in range(RELAY_SECTIONS):
        outputs.append(section_layer(gate_rows[section_pos], key_rows[section_pos], value_rows[section_pos], filters[section_pos], skip_gain))
    gated = jnp.stack(outputs)
    return jnp.roll(gated, 1, axis=0)
```

```python
import functools

import jax
import jax.numpy as jnp
from jax import lax
from jax.experimental import pallas as pl
from jax.experimental.pallas import tpu as pltpu
from jax.sharding import PartitionSpec as P

MESH = pl.DeviceIdType.MESH
LANES = 128


def kernel(
    n, sections, taps,
    gate_hbm, key_hbm, value_hbm, filt_hbm, skip_ref, out_hbm,
    gate_v, key_v, value_v, filt_v, turned, send_rows, taps_send, got_rows, got_taps,
    conv_send, conv_got, gated, acc_ref,
    load_sem, rows_ssem, rows_rsem, taps_ssem, taps_rsem,
    back_ssem, back_rsem, pass_ssem, pass_rsem, own_sem,
):
    rows = key_v.shape[0]
    groups = filt_v.shape[1]
    depth = key_v.shape[1] // groups
    halves = groups // LANES
    per = LANES // n
    me = lax.axis_index("ctx")
    sec = lax.axis_index("section")
    after = lax.rem(sec + 1, sections)
    before = lax.rem(sec + sections - 1, sections)

    loads = [
        pltpu.make_async_copy(src, dst, load_sem.at[i])
        for i, (src, dst) in enumerate(
            ((key_hbm, key_v), (value_hbm, value_v), (filt_hbm, filt_v), (gate_hbm, gate_v))
        )
    ]
    for load in loads:
        load.start()

    barrier = pltpu.get_barrier_semaphore()

    @pl.loop(1, n)
    def _(off):
        pl.semaphore_signal(
            barrier, inc=1, device_id={"ctx": lax.rem(me + off, n)}, device_id_type=MESH
        )

    pl.semaphore_signal(barrier, inc=1, device_id={"section": after}, device_id_type=MESH)
    pl.semaphore_signal(barrier, inc=1, device_id={"section": before}, device_id_type=MESH)

    @pl.loop(0, n)
    def _(p):
        for h in range(halves):
            got_rows[h, p] = jnp.zeros(got_rows.shape[2:], got_rows.dtype)

    loads[2].wait()
    for h in range(halves):
        block = filt_v[:, h * LANES:(h + 1) * LANES].astype(jnp.float32).T
        taps_send[h] = block.reshape(n, per, 1, LANES)
    loads[0].wait()
    loads[1].wait()

    def rows_copy(h, peer, slot):
        return pltpu.make_async_remote_copy(
            src_ref=send_rows.at[h, peer], dst_ref=got_rows.at[h, n + slot],
            send_sem=rows_ssem.at[h, peer], recv_sem=rows_rsem.at[h, slot],
            device_id={"ctx": peer}, device_id_type=MESH,
        )

    def taps_copy(peer, slot):
        return pltpu.make_async_remote_copy(
            src_ref=taps_send.at[:, peer], dst_ref=got_taps.at[slot],
            send_sem=taps_ssem.at[peer], recv_sem=taps_rsem.at[slot],
            device_id={"ctx": peer}, device_id_type=MESH,
        )

    def back_copy(h, peer, slot):
        return pltpu.make_async_remote_copy(
            src_ref=conv_send.at[h, peer], dst_ref=conv_got.at[h, slot],
            send_sem=back_ssem.at[h, peer], recv_sem=back_rsem.at[h, slot],
            device_id={"ctx": peer}, device_id_type=MESH,
        )

    def pass_copy(h, k):
        cols = pl.ds(k * groups + h * LANES, LANES)
        return pltpu.make_async_remote_copy(
            src_ref=gated.at[:, cols], dst_ref=out_hbm.at[:, cols],
            send_sem=pass_ssem.at[h, k], recv_sem=pass_rsem.at[h, k],
            device_id={"section": after}, device_id_type=MESH,
        )

    def mixed_of(h, k):
        cols = slice(k * groups + h * LANES, k * groups + (h + 1) * LANES)
        product = key_v[:, cols].astype(jnp.float32) * value_v[:, cols].astype(jnp.float32)
        return product.astype(jnp.bfloat16).astype(jnp.float32)

    def peers(body):
        @pl.loop(1, n)
        def _(off):
            body(lax.rem(me + off, n))

    own_taps = pltpu.make_async_copy(taps_send.at[:, me], got_taps.at[me], own_sem.at[0])
    own_rows = [
        pltpu.make_async_copy(send_rows.at[h, me], got_rows.at[h, n + me], own_sem.at[1 + h])
        for h in range(halves)
    ]
    own_back = [
        pltpu.make_async_copy(conv_send.at[h, me], conv_got.at[h, me], own_sem.at[1 + halves + h])
        for h in range(halves)
    ]

    for h in range(halves):
        for k in range(depth):
            turned[pl.ds(k, LANES, stride=depth), :] = mixed_of(h, k).T
        send_rows[h] = turned[...].astype(jnp.bfloat16).reshape(n, per, depth, rows)
        if h == 0:
            pl.semaphore_wait(barrier, n + 1)
            peers(lambda peer: taps_copy(peer, me).start())
            own_taps.start()
        peers(lambda peer: rows_copy(h, peer, me).start())
        own_rows[h].start()

    lane = lax.broadcasted_iota(jnp.int32, (rows, rows), 1)
    line = lax.broadcasted_iota(jnp.int32, (rows, rows), 0)
    upper = lane >= line

    def spread(row):
        return pltpu.roll(
            jnp.broadcast_to(row, (rows, rows)), 0, 1, stride=1, stride_axis=0
        )

    for h in range(halves):
        if h == 0:
            own_taps.wait()
            peers(lambda peer: taps_copy(me, peer).wait_recv())
        own_rows[h].wait()
        peers(lambda peer: rows_copy(h, me, peer).wait_recv())

        @pl.loop(0, per)
        def _(f):
            def piece(first, prev_row):
                prev = None if prev_row is None else spread(prev_row)
                blocks = []
                lhs = []
                for i in range(taps):
                    now = spread(got_taps[first + i, h, f])
                    low = jnp.zeros_like(now) if prev is None else prev
                    blocks.append(jnp.where(upper, now, low).astype(jnp.bfloat16))
                    prev = now
                    lhs.append(
                        got_rows[h, pl.ds(n - first - i, n), f].reshape(n * depth, rows)
                    )
                return jnp.dot(
                    jnp.concatenate(lhs, axis=1), jnp.concatenate(blocks, axis=0),
                    preferred_element_type=jnp.float32,
                )

            total = piece(0, None)
            if n > taps:
                acc_ref[...] = total

                @pl.loop(1, n // taps)
                def _(step):
                    first = step * taps
                    acc_ref[...] += piece(first, got_taps[first - 1, h, f])

                total = acc_ref[...]
            conv_send[h, :, f] = total.astype(jnp.bfloat16).reshape(n, depth, rows)

        peers(lambda peer: back_copy(h, peer, me).start())
        own_back[h].start()

    loads[3].wait()
    for h in range(halves):
        own_back[h].wait()
        peers(lambda peer: back_copy(h, me, peer).wait_recv())
        turned[...] = conv_got[h].reshape(LANES * depth, rows).astype(jnp.float32)
        for k in range(depth):
            cols = slice(k * groups + h * LANES, k * groups + (h + 1) * LANES)
            convolved = turned[pl.ds(k, LANES, stride=depth), :].T
            gated[:, cols] = (
                gate_v[:, cols].astype(jnp.float32)
                * (convolved + skip_ref[:, cols] * mixed_of(h, k))
            ).astype(jnp.bfloat16)
            pass_copy(h, k).start()

    for h in range(halves):
        for k in range(depth):
            pass_copy(h, k).wait()
    peers(lambda peer: taps_copy(peer, me).wait_send())
    for h in range(halves):
        peers(lambda peer: rows_copy(h, peer, me).wait_send())
        peers(lambda peer: back_copy(h, peer, me).wait_send())


def local(gate_rows, key_rows, value_rows, filters, skip_gain):
    n = lax.axis_size("ctx")
    sections = lax.axis_size("section")
    rows, channels = gate_rows.shape[1:]
    groups = filters.shape[2]
    depth = channels // groups
    halves = groups // LANES
    per = LANES // n
    bf16, f32 = jnp.bfloat16, jnp.float32
    hbm = pl.BlockSpec(memory_space=pl.ANY)
    dma = pltpu.SemaphoreType.DMA
    taps = min(n, 8)
    out = pl.pallas_call(
        functools.partial(kernel, n, sections, taps),
        out_shape=jax.ShapeDtypeStruct((rows, channels), bf16),
        in_specs=[hbm] * 4 + [pl.BlockSpec(memory_space=pltpu.VMEM)],
        out_specs=hbm,
        scratch_shapes=[
            pltpu.VMEM((rows, channels), bf16),
            pltpu.VMEM((rows, channels), bf16),
            pltpu.VMEM((rows, channels), bf16),
            pltpu.VMEM((rows, groups), bf16),
            pltpu.VMEM((LANES * depth, rows), f32),
            pltpu.VMEM((halves, n, per, depth, rows), bf16),
            pltpu.VMEM((halves, n, per, 1, rows), f32),
            pltpu.VMEM((halves, 2 * n, per, depth, rows), bf16),
            pltpu.VMEM((n, halves, per, 1, rows), f32),
            pltpu.VMEM((halves, n, per, depth, rows), bf16),
            pltpu.VMEM((halves, n, per, depth, rows), bf16),
            pltpu.VMEM((rows, channels), bf16),
            pltpu.VMEM((n * depth, rows), f32),
            dma((4,)),
            dma((halves, n)), dma((halves, n)),
            dma((n,)), dma((n,)),
            dma((halves, n)), dma((halves, n)),
            dma((halves, depth)), dma((halves, depth)),
            dma((1 + 2 * halves,)),
        ],
        compiler_params=pltpu.CompilerParams(
            collective_id=0, has_side_effects=True, vmem_limit_bytes=40 * 2**20
        ),
    )(gate_rows[0], key_rows[0], value_rows[0], filters[0], skip_gain[None])
    return out[None]


def solution(mesh):
    rows = P("section", "ctx", None)
    return jax.shard_map(
        local, mesh=mesh, in_specs=(rows, rows, rows, rows, P()), out_specs=rows,
        check_vma=False,
    )
```

```python
import functools

import jax
import jax.numpy as jnp
from jax import lax
from jax.experimental import pallas as pl
from jax.experimental.pallas import tpu as pltpu
from jax.sharding import PartitionSpec as P

MESH = pl.DeviceIdType.MESH
LANES = 128


def kernel(
    n, sections, pack, parts,
    gate_hbm, key_hbm, value_hbm, filt_hbm, skip_ref, out_hbm,
    gate_v, key_v, value_v, filt_v, turned, send_rows, taps_send, got_rows, got_taps,
    conv_send, conv_got, gated, tiles, acc_ref, skips,
    load_sem, rows_ssem, rows_rsem, taps_ssem, taps_rsem,
    back_ssem, back_rsem, pass_ssem, pass_rsem, own_sem,
):
    rows = key_v.shape[0]
    groups = filt_v.shape[1]
    depth = key_v.shape[1] // groups
    halves = groups // LANES
    per = LANES // n
    span = depth // pack
    sets = per // pack
    sub = sets // parts
    chunks = [(h, s) for h in range(halves) for s in range(pack)]
    taps = min(n, 8)
    me = lax.axis_index("ctx")
    sec = lax.axis_index("section")
    after = lax.rem(sec + 1, sections)
    before = lax.rem(sec + sections - 1, sections)

    loads = [
        pltpu.make_async_copy(src, dst, load_sem.at[i])
        for i, (src, dst) in enumerate(
            ((filt_hbm, filt_v), (key_hbm, key_v), (value_hbm, value_v), (gate_hbm, gate_v))
        )
    ]
    for load in loads:
        load.start()

    barrier = pltpu.get_barrier_semaphore()
    pl.semaphore_signal(barrier, inc=1, device_id={"section": before}, device_id_type=MESH)

    @pl.loop(1, n)
    def _(off):
        pl.semaphore_signal(
            barrier, inc=1, device_id={"ctx": lax.rem(me + off, n)}, device_id_type=MESH
        )

    @pl.loop(0, n)
    def _(p):
        for c in range(len(chunks)):
            got_rows[c, p] = jnp.zeros(got_rows.shape[2:], got_rows.dtype)

    for k in range(depth):
        skips[k:k + 1, :] = skip_ref[:, k * groups:(k + 1) * groups]

    def rows_copy(c, j, peer, slot):
        part = pl.ds(j * sub, sub)
        return pltpu.make_async_remote_copy(
            src_ref=send_rows.at[c, peer, part], dst_ref=got_rows.at[c, n + slot, part],
            send_sem=rows_ssem.at[c, j, peer], recv_sem=rows_rsem.at[c, j, slot],
            device_id={"ctx": peer}, device_id_type=MESH,
        )

    def taps_copy(h, peer, slot):
        return pltpu.make_async_remote_copy(
            src_ref=taps_send.at[h, peer], dst_ref=got_taps.at[h, slot],
            send_sem=taps_ssem.at[h, peer], recv_sem=taps_rsem.at[h, slot],
            device_id={"ctx": peer}, device_id_type=MESH,
        )

    def back_copy(c, j, peer, slot):
        part = pl.ds(j * sub, sub)
        return pltpu.make_async_remote_copy(
            src_ref=conv_send.at[c, peer, part], dst_ref=conv_got.at[c, slot, part],
            send_sem=back_ssem.at[c, j, peer], recv_sem=back_rsem.at[c, j, slot],
            device_id={"ctx": peer}, device_id_type=MESH,
        )

    def pass_copy(h, k):
        cols = pl.ds(k * groups + h * LANES, LANES)
        return pltpu.make_async_remote_copy(
            src_ref=gated.at[:, cols], dst_ref=out_hbm.at[:, cols],
            send_sem=pass_ssem.at[h, k], recv_sem=pass_rsem.at[h, k],
            device_id={"section": after}, device_id_type=MESH,
        )

    def own_taps(h):
        return pltpu.make_async_copy(taps_send.at[h, me], got_taps.at[h, me], own_sem.at[0, h])

    def own_rows(c):
        return pltpu.make_async_copy(
            send_rows.at[c, me], got_rows.at[c, n + me], own_sem.at[1, c]
        )

    def own_back(c):
        return pltpu.make_async_copy(conv_send.at[c, me], conv_got.at[c, me], own_sem.at[2, c])

    def others(body):
        @pl.loop(1, n)
        def _(off):
            body(lax.rem(me + off, n))

    def turn(c):
        h, s = chunks[c]
        for i in range(span):
            first = (s * span + i) * groups + h * LANES
            cols = slice(first, first + LANES)
            product = key_v[:, cols].astype(jnp.float32) * value_v[:, cols].astype(jnp.float32)
            product = product.astype(jnp.bfloat16).astype(jnp.float32)
            turned[pl.ds(i, LANES, stride=span), :] = product.T
        send_rows[c] = turned[...].astype(jnp.bfloat16).reshape(n, sets, pack * span, rows)

    def send(c):
        for j in range(parts):
            others(lambda peer: rows_copy(c, j, peer, me).start())
        own_rows(c).start()

    loads[0].wait()
    for h in range(halves):
        block = filt_v[:, h * LANES:(h + 1) * LANES].astype(jnp.float32).T
        taps_send[h] = block.reshape(n, per, 1, LANES)
    loads[1].wait()
    loads[2].wait()
    turn(0)
    pl.semaphore_wait(barrier, n)
    others(lambda peer: taps_copy(0, peer, me).start())
    own_taps(0).start()
    send(0)
    for h in range(1, halves):
        others(lambda peer: taps_copy(h, peer, me).start())
        own_taps(h).start()
    for c in range(1, pack):
        turn(c)
        send(c)

    lane = lax.broadcasted_iota(jnp.int32, (rows, rows), 1)
    line = lax.broadcasted_iota(jnp.int32, (rows, rows), 0)
    upper = lane >= line
    slot_lane = lax.broadcasted_iota(jnp.int32, (depth, LANES), 1)

    def spread(row):
        return pltpu.roll(
            jnp.broadcast_to(row, (rows, rows)), 0, 1, stride=1, stride_axis=0
        )

    def build(h):
        own_taps(h).wait()
        others(lambda peer: taps_copy(h, me, peer).wait_recv())

        @pl.loop(0, sets)
        def _(g):
            for a in range(pack):
                f = g * pack + a

                def stretch(first, prev):
                    for i in range(taps):
                        now = spread(got_taps[h, first + i, f])
                        low = jnp.zeros_like(now) if prev is None else prev
                        tiles[h, g, first + i, :, a * LANES:(a + 1) * LANES] = jnp.where(
                            upper, now, low
                        ).astype(jnp.bfloat16)
                        prev = now

                stretch(0, None)
                if n > taps:
                    @pl.loop(1, n // taps)
                    def _(step):
                        stretch(step * taps, spread(got_taps[h, step * taps - 1, f]))

    def convolve(c):
        h, s = chunks[c]
        own_rows(c).wait()

        def one(g):
            def piece(first):
                lhs = [
                    got_rows[c, pl.ds(n - first - i, n), g].reshape(n * pack * span, rows)
                    for i in range(taps)
                ]
                weights = tiles[h, g, pl.ds(first, taps)].reshape(taps * rows, pack * LANES)
                return jnp.dot(
                    jnp.concatenate(lhs, axis=1), weights,
                    preferred_element_type=jnp.float32,
                )

            total = piece(0)
            if n > taps:
                acc_ref[...] = total

                @pl.loop(1, n // taps)
                def _(step):
                    acc_ref[...] += piece(step * taps)

                total = acc_ref[...]
            total = total.reshape(n, pack, span, pack * LANES)
            own = got_rows[c, n:, g].astype(jnp.float32).reshape(n, pack, span, rows)
            gains = skips[:, h * LANES:(h + 1) * LANES]
            done = []
            for a in range(pack):
                gain = jnp.sum(
                    jnp.where(slot_lane == me * per + g * pack + a, gains, 0.0),
                    axis=1, keepdims=True,
                )[s * span:(s + 1) * span]
                done.append(
                    total[:, a, :, a * LANES:(a + 1) * LANES] + gain[None] * own[:, a]
                )
            conv_send[c, :, g] = jnp.concatenate(done, axis=1).astype(jnp.bfloat16)

        for j in range(parts):
            others(lambda peer: rows_copy(c, j, me, peer).wait_recv())
            pl.loop(j * sub, (j + 1) * sub)(one)
            others(lambda peer: back_copy(c, j, peer, me).start())
        own_back(c).start()

    def finish(c):
        h, s = chunks[c]
        own_back(c).wait()
        for j in range(parts):
            others(lambda peer: back_copy(c, j, me, peer).wait_recv())
        turned[...] = conv_got[c].reshape(LANES * span, rows).astype(jnp.float32)
        for i in range(span):
            k = s * span + i
            cols = slice(k * groups + h * LANES, k * groups + (h + 1) * LANES)
            convolved = turned[pl.ds(i, LANES, stride=span), :].T
            gated[:, cols] = (gate_v[:, cols].astype(jnp.float32) * convolved).astype(
                jnp.bfloat16
            )
            pass_copy(h, k).start()

    build(0)
    for c in range(pack):
        convolve(c)
    for c in range(pack, len(chunks)):
        turn(c)
        send(c)
    loads[3].wait()
    finish(0)
    for h in range(1, halves):
        build(h)
    for c in range(1, pack):
        finish(c)
    for c in range(pack, len(chunks)):
        convolve(c)
    for c in range(pack, len(chunks)):
        finish(c)

    for h in range(halves):
        for k in range(depth):
            pass_copy(h, k).wait()
        others(lambda peer: taps_copy(h, peer, me).wait_send())
    for c in range(len(chunks)):
        for j in range(parts):
            others(lambda peer: rows_copy(c, j, peer, me).wait_send())
            others(lambda peer: back_copy(c, j, peer, me).wait_send())


def local(gate_rows, key_rows, value_rows, filters, skip_gain):
    n = lax.axis_size("ctx")
    sections = lax.axis_size("section")
    rows, channels = gate_rows.shape[1:]
    groups = filters.shape[2]
    depth = channels // groups
    halves = groups // LANES
    per = LANES // n
    bf16, f32 = jnp.bfloat16, jnp.float32
    hbm = pl.BlockSpec(memory_space=pltpu.HBM)
    dma = pltpu.SemaphoreType.DMA
    pack = 2 if per % 2 == 0 and depth % 16 == 0 else 1
    span, sets, chunks = depth // pack, per // pack, halves * pack
    parts = 2 if sets % 2 == 0 else 1
    out = pl.pallas_call(
        functools.partial(kernel, n, sections, pack, parts),
        out_shape=jax.ShapeDtypeStruct((rows, channels), bf16),
        in_specs=[hbm] * 4 + [pl.BlockSpec(memory_space=pltpu.VMEM)],
        out_specs=hbm,
        scratch_shapes=[
            pltpu.VMEM((rows, channels), bf16),
            pltpu.VMEM((rows, channels), bf16),
            pltpu.VMEM((rows, channels), bf16),
            pltpu.VMEM((rows, groups), bf16),
            pltpu.VMEM((LANES * span, rows), f32),
            pltpu.VMEM((chunks, n, sets, depth, rows), bf16),
            pltpu.VMEM((halves, n, per, 1, rows), f32),
            pltpu.VMEM((chunks, 2 * n, sets, depth, rows), bf16),
            pltpu.VMEM((halves, n, per, 1, rows), f32),
            pltpu.VMEM((chunks, n, sets, depth, rows), bf16),
            pltpu.VMEM((chunks, n, sets, depth, rows), bf16),
            pltpu.VMEM((rows, channels), bf16),
            pltpu.VMEM((halves, sets, n, rows, pack * LANES), bf16),
            pltpu.VMEM((n * depth, pack * LANES), f32),
            pltpu.VMEM((depth, groups), f32),
            dma((4,)),
            dma((chunks, parts, n)), dma((chunks, parts, n)),
            dma((halves, n)), dma((halves, n)),
            dma((chunks, parts, n)), dma((chunks, parts, n)),
            dma((halves, depth)), dma((halves, depth)),
            dma((3, chunks)),
        ],
        compiler_params=pltpu.CompilerParams(
            collective_id=0, has_side_effects=True, vmem_limit_bytes=60 * 2**20
        ),
    )(gate_rows[0], key_rows[0], value_rows[0], filters[0], skip_gain[None])
    return out[None]


def solution(mesh):
    rows = P("section", "ctx", None)
    return jax.shard_map(
        local, mesh=mesh, in_specs=(rows, rows, rows, rows, P()), out_specs=rows,
        check_vma=False,
    )
```
